32 devices in a mesh: box: 32 (over z, y, x, core).
Axes of the slice: x: 2, y: 2, z: 4, core: 2. Of those that a mesh axis runs over, the one named last changes fastest.
Arguments:
- fine_multipoles: bfloat16 [152, 16384], P(None, 'box'), may hold values from -6 to 6
- present: int32 [16384], P('box'), may hold values from 0 to 1, as said below
- m2m_ops: bfloat16 [8, 152, 152], replicated, may hold values from -0.15625 to 0.15625
- m2l_ops: bfloat16 [316, 152, 152], replicated, may hold values from -0.0390625 to 0.0390625
- l2l_ops: bfloat16 [8, 152, 152], replicated, may hold values from -0.5 to 0.5
Outputs:
- fine_locals: float32 [152, 16384], P(None, 'box')
The draws below stay inside these ranges and needn't reach their ends.
Inputs may be any that keep to these rules, and one draw needn't show every extreme that they name: `present`: the column of fine_multipoles of a box marked 0 holds no data and is not read.
All inputs are finite; a program needn't handle non-finite values.
Results may differ from the reference program's by a relative error of at most 0.0027.
Values may be sent and summed in bfloat16 or wider, within the bound.
A program may use at most 384 MiB of HBM per device.

```python
import jax
import jax.numpy as jnp
import numpy as np
from jax import lax

P_SIZE = 152
NT = 316
BOXES = 16384


def draw_present(key, part):
    keys = jax.random.split(jax.random.fold_in(key, 5), 2)
    levels = jax.random.randint(keys[0], (BOXES // 64,), 30, 97, dtype=jnp.int32)
    chances = jnp.repeat(levels, 64)
    rolls = jax.random.randint(keys[1], (BOXES,), 0, 100, dtype=jnp.int32)
    return (rolls < chances).astype(jnp.int32)


def block_levels(stream_key, dims, shards, smallest, top_value):
    gain = 1.0
    for dim, shards_of in shards:
        draws = jax.random.uniform(jax.random.fold_in(jax.random.fold_in(stream_key, 6), dim), (shards_of,), jnp.float32, smallest / len(shards), top_value / len(shards))
        gain = gain * jnp.repeat(jnp.exp(draws), dims[dim] // shards_of).reshape((-1,) + (1,) * (len(dims) - 1 - dim))
    return gain


def normal_values(rng, shape, scale, reach, shards=(), kind=jnp.bfloat16):
    values = jax.random.normal(rng, shape, jnp.float32) * scale
    if len(shards) > 0:
        values = block_levels(rng, shape, shards, -0.22, 0.18) * values
    return jnp.clip(values, min=-reach, max=reach).astype(kind)


def setup_inputs(seed: int = 0) -> dict:
    key_of = jax.random.split(jax.random.key(seed), 6)
    fine_multipoles = normal_values(key_of[0], (P_SIZE, BOXES), 1.0, 6.0, ((1, 32),))
    present = draw_present(jax.random.fold_in(key_of[5], 71), 0)
    m2m_ops = normal_values(key_of[2], (8, P_SIZE, P_SIZE), (8 * P_SIZE) ** -0.5, 0.15625)
    m2l_ops = normal_values(key_of[3], (NT, P_SIZE, P_SIZE), (128 * P_SIZE) ** -0.5, 0.0390625)
    l2l_ops = normal_values(key_of[4], (8, P_SIZE, P_SIZE), P_SIZE ** -0.5, 0.5)
    return {"fine_multipoles": fine_multipoles, "present": present, "m2m_ops": m2m_ops, "m2l_ops": m2l_ops, "l2l_ops": l2l_ops}


def offsets_table():
    entries = []
    for along_x in range(-3, 4):
        for along_y in range(-3, 4):
            for along_z in range(-3, 4):
                if max(abs(along_x), abs(along_y), abs(along_z)) >= 2:
                    entries.append((along_x, along_y, along_z))
    return entries


def axis_members(bit_count):
    return [[bit_level for bit_level in range(bit_count) if bit_level % 3 == axis_number][::-1]
            for axis_number in range(3)]


def to_grid(columns, bit_count):
    leading = columns.shape[:-1]
    lead_count = len(leading)
    bitwise = columns.reshape(leading + (2,) * bit_count)
    ordering = list(range(lead_count))
    extent = []
    for members in axis_members(bit_count):
        ordering += [lead_count + bit_count - 1 - member for member in members]
        extent.append(2 ** len(members))
    return jnp.transpose(bitwise, ordering).reshape(leading + tuple(extent))


def from_grid(field_grid, bit_count):
    leading = field_grid.shape[:-3]
    lead_count = len(leading)
    bitwise = field_grid.reshape(leading + (2,) * bit_count)
    ordering = []
    for members in axis_members(bit_count):
        ordering += [bit_count - 1 - member for member in members]
    inverse = [0] * bit_count
    for position, anchor in enumerate(ordering):
        inverse[anchor] = position
    permuted = list(range(lead_count)) + [lead_count + position for position in inverse]
    return jnp.transpose(bitwise, permuted).reshape(leading + (2 ** bit_count,))


def upward(children, m2m_ops):
    grouped = children.astype(jnp.float32).reshape(children.shape[0], children.shape[1] // 8, 8)
    return jnp.einsum('kpq,qck->pc', m2m_ops.astype(jnp.float32), grouped).astype(jnp.bfloat16)


def parity_keep(offset, coords):
    even_flag = (coords % 2) == 0
    return jnp.where(offset == 3, even_flag, jnp.where(offset == -3, jnp.logical_not(even_flag), coords >= 0))


def translate(field_grid, m2l_ops):
    size_x, size_y, size_z, points = field_grid.shape
    padded = jnp.pad(field_grid, ((3, 3), (3, 3), (3, 3), (0, 0)))
    coord_x = jnp.arange(size_x, dtype=jnp.int32)[:, None, None]
    coord_y = jnp.arange(size_y, dtype=jnp.int32)[None, :, None]
    coord_z = jnp.arange(size_z, dtype=jnp.int32)[None, None, :]
    offsets = jnp.asarray(np.array(offsets_table(), dtype=np.int32))

    def advance(totals, inputs):
        operator, offset = inputs
        window = lax.dynamic_slice(padded, (offset[0] + 3, offset[1] + 3, offset[2] + 3, jnp.int32(0)),
                                   (size_x, size_y, size_z, points))
        keeping = parity_keep(offset[0], coord_x) & parity_keep(offset[1], coord_y) & parity_keep(offset[2], coord_z)
        product_term = jnp.dot(window.reshape(-1, points), operator.T, preferred_element_type=jnp.float32)
        return totals + product_term * keeping.reshape(-1, 1).astype(jnp.float32), None

    start = jnp.zeros((size_x * size_y * size_z, points), jnp.float32)
    totals, _ = lax.scan(advance, start, (m2l_ops, offsets))
    return totals.reshape(size_x, size_y, size_z, points)


def reference(fine_multipoles, present, m2m_ops, m2l_ops, l2l_ops):
    bit_count = BOXES.bit_length() - 1
    points = fine_multipoles.shape[0]
    masked = jnp.where(present[None, :] > 0, fine_multipoles, jnp.zeros_like(fine_multipoles))
    coarse = upward(masked, m2m_ops)
    fine_grid = jnp.moveaxis(to_grid(masked, bit_count), 0, -1)
    coarse_grid = jnp.moveaxis(to_grid(coarse, bit_count - 3), 0, -1)
    fine_down = from_grid(jnp.moveaxis(translate(fine_grid, m2l_ops), -1, 0), bit_count)
    coarse_down = translate(coarse_grid, m2l_ops).astype(jnp.bfloat16)
    coarse_down = from_grid(jnp.moveaxis(coarse_down, -1, 0), bit_count - 3)
    spread = jnp.einsum('kpq,qc->pck', l2l_ops.astype(jnp.float32), coarse_down.astype(jnp.float32))
    return jnp.where(present[None, :] > 0, fine_down + spread.reshape(points, BOXES), 0.0)
```

```python
import functools

import jax
import jax.numpy as jnp
import numpy as np
from jax import lax
from jax.experimental import pallas as pl
from jax.experimental.pallas import tpu as pltpu
from jax.sharding import PartitionSpec as P

PAD = 16
NT_DIMS = (((1,), (1,)), ((), ()))


def offsets_table():
    entries = []
    for u in range(-3, 4):
        for v in range(-3, 4):
            for w in range(-3, 4):
                if max(abs(u), abs(v), abs(w)) >= 2:
                    entries.append((u, v, w))
    return entries


def coords_of(number, bit_count):
    out = [0, 0, 0]
    for i in range(bit_count):
        out[i % 3] |= (number >> i & 1) << (i // 3)
    return out


def extents(bit_count):
    return [2 ** len([i for i in range(bit_count) if i % 3 == a]) for a in range(3)]


def kind(o):
    return {-3: 0, 3: 2}.get(o, 1)


def classes_of(kinds):
    allowed = {0: (1,), 1: (0, 1), 2: (0,)}
    return [
        k
        for k in range(8)
        if all((k >> a & 1) in allowed[kinds[a]] for a in range(3))
    ]


def build_tables():
    offsets = offsets_table()
    rows, starts, slabs = [], [], []
    for u in range(-3, 4):
        members = [t for t, o in enumerate(offsets) if o[0] == u]
        slabs.append((members[0], len(members)))
        for kv in range(3):
            for kw in range(3):
                starts.append(len(rows))
                for t in members:
                    o = offsets[t]
                    if kind(o[1]) != kv or kind(o[2]) != kw:
                        continue
                    entry = [t]
                    for k in classes_of((kind(u), kv, kw)):
                        d, child = 0, 0
                        for a in range(3):
                            s = o[a] + (k >> a & 1)
                            child |= (s & 1) << a
                            d = d * 3 + (s >> 1) + 1
                        entry.append(d * 8 + child)
                    rows.append(entry + [0] * (9 - len(entry)))
    starts.append(len(rows))
    return np.array(rows, np.int32).reshape(-1), np.array(starts, np.int32), slabs


def selector(bit_count, pad):
    ex = extents(bit_count)
    count = 2**bit_count
    rows = max(count, pad)
    sel = np.zeros((27, rows, (ex[0] + 2) * (ex[1] + 2) * (ex[2] + 2)), np.float32)
    for c in range(count):
        x = coords_of(c, bit_count)
        r = (c & 7) * (count // 8) + (c >> 3) if count >= 64 else c
        for d in range(27):
            s = [x[0] + d // 9, x[1] + d // 3 % 3, x[2] + d % 3]
            sel[d, r, (s[0] * (ex[1] + 2) + s[1]) * (ex[2] + 2) + s[2]] = 1
    return sel.reshape(27 * rows, -1)


def far_kernel(
    slabs, nf, nc, tab_ref, start_ref, fine_ref, coarse_ref, sf_ref, sc_ref, l2l_ref, m2l_ref,
    out_ref, ops, win, acc, sems
):
    copies = []
    for i, (first, size) in enumerate(slabs):
        copy = pltpu.make_async_copy(
            m2l_ref.at[pl.ds(first, size)], ops.at[pl.ds(first, size)], sems.at[i]
        )
        copy.start()
        copies.append(copy)
    acc[...] = jnp.zeros_like(acc)
    points = fine_ref.shape[-1]

    def build(j, carry):
        f = fine_ref[j]
        c = coarse_ref[j]
        for d in range(27):
            win[d * 8 + j, 0:nf, :] = jnp.dot(
                sf_ref[d * nf : (d + 1) * nf, :], f, preferred_element_type=jnp.float32
            ).astype(jnp.bfloat16)
            win[d * 8 + j, nf : nf + PAD, :] = jnp.dot(
                sc_ref[d * PAD : (d + 1) * PAD, :], c, preferred_element_type=jnp.float32
            ).astype(jnp.bfloat16)
        return carry

    lax.fori_loop(0, 8, build, 0)
    rows = nf + PAD

    def slab(i, ku):
        for kv in range(3):
            for kw in range(3):
                ks = classes_of((ku, kv, kw))

                def step(n, carry, ks=ks):
                    op = ops[tab_ref[n * 9]]
                    lhs = jnp.concatenate(
                        [win[tab_ref[n * 9 + 1 + e]] for e in range(len(ks))], axis=0
                    )
                    res = lax.dot_general(lhs, op, NT_DIMS, preferred_element_type=jnp.float32)
                    for e, k in enumerate(ks):
                        acc[k] += res[e * rows : (e + 1) * rows]
                    return carry

                at = i * 9 + kv * 3 + kw
                lax.fori_loop(start_ref[at], start_ref[at + 1], step, 0)

    copies[0].wait()
    slab(0, 0)
    for i in range(1, 6):
        copies[i].wait()

    def inner(i, carry):
        slab(i, 1)
        return carry

    lax.fori_loop(1, 6, inner, 0)
    copies[6].wait()
    slab(6, 2)

    down = jnp.concatenate([acc[k, nf : nf + nc, :] for k in range(8)], axis=0).astype(jnp.bfloat16)
    for k in range(8):
        out_ref[k] = acc[k, 0:nf, :] + lax.dot_general(
            down, l2l_ref[k], NT_DIMS, preferred_element_type=jnp.float32
        )


def far_field(fine, coarse, m2l_ops, l2l_ops, nf, nc, local_bits):
    tab, starts, slabs = build_tables()
    points = fine.shape[-1]
    sf = jnp.asarray(selector(local_bits - 3, 0), jnp.bfloat16)
    sc = jnp.asarray(selector(local_bits - 6, PAD), jnp.bfloat16)
    vmem = pl.BlockSpec(memory_space=pltpu.VMEM)
    smem = pl.BlockSpec(memory_space=pltpu.SMEM)
    return pl.pallas_call(
        functools.partial(far_kernel, slabs, nf, nc),
        out_shape=jax.ShapeDtypeStruct((8, nf, points), jnp.float32),
        in_specs=[smem, smem, vmem, vmem, vmem, vmem, vmem, pl.BlockSpec(memory_space=pl.ANY)],
        out_specs=vmem,
        scratch_shapes=[
            pltpu.VMEM(m2l_ops.shape, jnp.bfloat16),
            pltpu.VMEM((27 * 8, nf + PAD, points), jnp.bfloat16),
            pltpu.VMEM((8, nf + PAD, points), jnp.float32),
            pltpu.SemaphoreType.DMA((len(slabs),)),
        ],
        compiler_params=pltpu.CompilerParams(vmem_limit_bytes=60 * 2**20),
        name="far_field",
    )(jnp.asarray(tab), jnp.asarray(starts), fine, coarse, sf, sc, l2l_ops, m2l_ops)


def to_grid(boxes, bit_count):
    lead, count, points = boxes.shape
    bitwise = boxes.reshape((lead,) + (2,) * bit_count + (points,))
    order = [0]
    for a in range(3):
        order += [bit_count - i for i in range(bit_count) if i % 3 == a][::-1]
    return bitwise.transpose(order + [bit_count + 1]).reshape([lead] + extents(bit_count) + [points])


def neighbours(devices, device_bits, local_bits, axis):
    members = [p for p in range(device_bits) if (local_bits + p) % 3 == axis]
    pairs = []
    for i in range(devices):
        coord = sum((i >> p & 1) << n for n, p in enumerate(members))
        if coord + 1 < 2 ** len(members):
            j = i
            for n, p in enumerate(members):
                j = j & ~(1 << p) | ((coord + 1) >> n & 1) << p
            pairs.append((i, j))
    return pairs


def exchange(grids, devices, device_bits, local_bits):
    for axis in range(3):
        up = neighbours(devices, device_bits, local_bits, axis)
        down = [(j, i) for i, j in up]
        dim = axis + 1

        def faces(at_top):
            cut = []
            for g in grids:
                s = g.shape[dim] - 1 if at_top else 0
                face = lax.slice_in_dim(g, s, s + 1, axis=dim)
                cut.append(face.reshape(g.shape[0], -1, g.shape[-1]))
            return jnp.concatenate(cut, axis=1)

        below = lax.ppermute(faces(True), "box", up)
        above = lax.ppermute(faces(False), "box", down)
        out, at = [], 0
        for g in grids:
            shape = list(g.shape)
            shape[dim] = 1
            size = shape[1] * shape[2] * shape[3]
            out.append(
                jnp.concatenate(
                    [
                        below[:, at : at + size].reshape(shape),
                        g,
                        above[:, at : at + size].reshape(shape),
                    ],
                    axis=dim,
                )
            )
            at += size
        grids = out
    return grids


def shards(fine_multipoles, present, m2m_ops, m2l_ops, l2l_ops):
    points, width = fine_multipoles.shape
    local_bits = width.bit_length() - 1
    devices = lax.axis_size("box")
    device_bits = devices.bit_length() - 1
    nf, nc = width // 8, width // 64
    masked = jnp.where(present[None, :] > 0, fine_multipoles, jnp.zeros_like(fine_multipoles))
    fine = masked.reshape(points, nf, 8).transpose(2, 1, 0)
    coarse = jnp.einsum(
        "kcq,kpq->cp", fine, m2m_ops, preferred_element_type=jnp.float32
    ).astype(jnp.bfloat16)
    coarse = coarse.reshape(nc, 8, points).transpose(1, 0, 2)
    grids = exchange(
        [to_grid(fine, local_bits - 3), to_grid(coarse, local_bits - 6)],
        devices, device_bits, local_bits,
    )
    flat = [g.reshape(8, -1, points) for g in grids]
    rows = far_field(flat[0], flat[1], m2l_ops, l2l_ops, nf, nc, local_bits)
    out = rows.reshape(8, 8, nc, points).transpose(3, 2, 1, 0).reshape(points, width)
    return jnp.where(present[None, :] > 0, out, 0.0)


def solution(mesh):
    in_specs = (P(None, "box"), P("box"), P(), P(), P())
    out_specs = P(None, "box")
    return jax.shard_map(shards, mesh=mesh, in_specs=in_specs, out_specs=out_specs, check_vma=False)
```

```python
import functools

import jax
import jax.numpy as jnp
import numpy as np
from jax import lax
from jax.experimental import pallas as pl
from jax.experimental.pallas import tpu as pltpu
from jax.sharding import PartitionSpec as P

PAD = 16
GROUPS = ((8, 7), (4, 5), (2, 5), (1, 1))
SLABS = 8
NT_DIMS = (((1,), (1,)), ((), ()))


def offsets_table():
    entries = []
    for u in range(-3, 4):
        for v in range(-3, 4):
            for w in range(-3, 4):
                if max(abs(u), abs(v), abs(w)) >= 2:
                    entries.append((u, v, w))
    return entries


def coords_of(number, bit_count):
    out = [0, 0, 0]
    for i in range(bit_count):
        out[i % 3] |= (number >> i & 1) << (i // 3)
    return out


def extents(bit_count):
    return [2 ** len([i for i in range(bit_count) if i % 3 == a]) for a in range(3)]


def kind(o):
    return {-3: 0, 3: 2}.get(o, 1)


def classes_of(kinds):
    allowed = {0: (1,), 1: (0, 1), 2: (0,)}
    return [
        k
        for k in range(8)
        if all((k >> a & 1) in allowed[kinds[a]] for a in range(3))
    ]


def build_tables():
    offsets = offsets_table()
    tables = []
    for classes, together in GROUPS:
        rows = []
        for kinds in np.ndindex(3, 3, 3):
            ks = classes_of(kinds)
            if len(ks) != classes:
                continue
            members = [t for t, o in enumerate(offsets) if tuple(map(kind, o)) == kinds]
            for first in range(0, len(members), together):
                entry = list(ks)
                for t in members[first : first + together]:
                    entry.append(t)
                    for k in ks:
                        d, child = 0, 0
                        for a in range(3):
                            s = offsets[t][a] + (k >> a & 1)
                            child |= (s & 1) << a
                            d = d * 3 + (s >> 1) + 1
                        entry.append(d * 8 + child)
                rows.append(entry)
        tables.append(np.array(rows, np.int32))
    return tables


def selector(bit_count, pad):
    ex = extents(bit_count)
    count = 2**bit_count
    rows = max(count, pad)
    sel = np.zeros((27, rows, (ex[0] + 2) * (ex[1] + 2) * (ex[2] + 2)), np.float32)
    for c in range(count):
        x = coords_of(c, bit_count)
        r = (c & 7) * (count // 8) + (c >> 3) if count >= 64 else c
        for d in range(27):
            s = [x[0] + d // 9, x[1] + d // 3 % 3, x[2] + d % 3]
            sel[d, r, (s[0] * (ex[1] + 2) + s[1]) * (ex[2] + 2) + s[2]] = 1
    return sel.reshape(27 * rows, -1)


def far_kernel(
    layout, nf, nc, tab_ref, fine_ref, coarse_ref, sf_ref, sc_ref, l2l_ref, m2l_ref,
    out_ref, ops, win, acc, sems
):
    total = ops.shape[0]
    copies = []
    for i in range(SLABS):
        at, end = total * i // SLABS, total * (i + 1) // SLABS
        copy = pltpu.make_async_copy(
            m2l_ref.at[pl.ds(at, end - at)], ops.at[pl.ds(at, end - at)], sems.at[i]
        )
        copy.start()
        copies.append(copy)
    acc[...] = jnp.zeros_like(acc)

    def build(j, carry):
        f = fine_ref[j]
        c = coarse_ref[j]
        for d in range(27):
            win[d * 8 + j, 0:nf, :] = jnp.dot(
                sf_ref[d * nf : (d + 1) * nf, :], f, preferred_element_type=jnp.float32
            ).astype(jnp.bfloat16)
            win[d * 8 + j, nf : nf + PAD, :] = jnp.dot(
                sc_ref[d * PAD : (d + 1) * PAD, :], c, preferred_element_type=jnp.float32
            ).astype(jnp.bfloat16)
        return carry

    lax.fori_loop(0, 8, build, 0)
    rows = nf + PAD

    for copy in copies:
        copy.wait()

    def apply(base, classes, together):
        sums = None
        for j in range(together):
            at = base + classes + j * (classes + 1)
            lhs = [win[tab_ref[at + 1 + e]] for e in range(classes)]
            lhs = jnp.concatenate(lhs, axis=0) if classes > 1 else lhs[0]
            term = lax.dot_general(
                lhs, ops[tab_ref[at]], NT_DIMS, preferred_element_type=jnp.float32
            )
            sums = term if sums is None else sums + term
        for e in range(classes):
            acc[tab_ref[base + e]] += sums[e * rows : (e + 1) * rows]

    for first, count, width, classes, together in layout:

        def step(n, carry, first=first, width=width, classes=classes, together=together):
            apply(first + n * width, classes, together)
            return carry

        lax.fori_loop(0, count, step, 0)

    down = jnp.concatenate([acc[k, nf : nf + nc, :] for k in range(8)], axis=0).astype(jnp.bfloat16)
    for k in range(8):
        out_ref[k] = acc[k, 0:nf, :] + lax.dot_general(
            down, l2l_ref[k], NT_DIMS, preferred_element_type=jnp.float32
        )


def far_field(fine, coarse, m2l_ops, l2l_ops, nf, nc, local_bits):
    tables = build_tables()
    layout, at = [], 0
    for table, (classes, together) in zip(tables, GROUPS):
        layout.append((at,) + table.shape + (classes, together))
        at += table.size
    tab = np.concatenate([table.reshape(-1) for table in tables])
    points = fine.shape[-1]
    sf = jnp.asarray(selector(local_bits - 3, 0), jnp.bfloat16)
    sc = jnp.asarray(selector(local_bits - 6, PAD), jnp.bfloat16)
    vmem = pl.BlockSpec(memory_space=pltpu.VMEM)
    smem = pl.BlockSpec(memory_space=pltpu.SMEM)
    return pl.pallas_call(
        functools.partial(far_kernel, layout, nf, nc),
        out_shape=jax.ShapeDtypeStruct((8, nf, points), jnp.float32),
        in_specs=[smem, vmem, vmem, vmem, vmem, vmem, pl.BlockSpec(memory_space=pl.ANY)],
        out_specs=vmem,
        scratch_shapes=[
            pltpu.VMEM(m2l_ops.shape, jnp.bfloat16),
            pltpu.VMEM((27 * 8, nf + PAD, points), jnp.bfloat16),
            pltpu.VMEM((8, nf + PAD, points), jnp.float32),
            pltpu.SemaphoreType.DMA((SLABS,)),
        ],
        compiler_params=pltpu.CompilerParams(vmem_limit_bytes=60 * 2**20),
        name="far_field",
    )(jnp.asarray(tab), fine, coarse, sf, sc, l2l_ops, m2l_ops)


def to_grid(boxes, bit_count):
    lead, count, points = boxes.shape
    bitwise = boxes.reshape((lead,) + (2,) * bit_count + (points,))
    order = [0]
    for a in range(3):
        order += [bit_count - i for i in range(bit_count) if i % 3 == a][::-1]
    return bitwise.transpose(order + [bit_count + 1]).reshape([lead] + extents(bit_count) + [points])


def neighbours(devices, device_bits, local_bits, axis):
    members = [p for p in range(device_bits) if (local_bits + p) % 3 == axis]
    pairs = []
    for i in range(devices):
        coord = sum((i >> p & 1) << n for n, p in enumerate(members))
        if coord + 1 < 2 ** len(members):
            j = i
            for n, p in enumerate(members):
                j = j & ~(1 << p) | ((coord + 1) >> n & 1) << p
            pairs.append((i, j))
    return pairs


def exchange(grids, devices, device_bits, local_bits):
    for axis in range(3):
        up = neighbours(devices, device_bits, local_bits, axis)
        down = [(j, i) for i, j in up]
        dim = axis + 1

        def faces(at_top):
            cut = []
            for g in grids:
                s = g.shape[dim] - 1 if at_top else 0
                face = lax.slice_in_dim(g, s, s + 1, axis=dim)
                cut.append(face.reshape(g.shape[0], -1, g.shape[-1]))
            return jnp.concatenate(cut, axis=1)

        below = lax.ppermute(faces(True), "box", up)
        above = lax.ppermute(faces(False), "box", down)
        out, at = [], 0
        for g in grids:
            shape = list(g.shape)
            shape[dim] = 1
            size = shape[1] * shape[2] * shape[3]
            out.append(
                jnp.concatenate(
                    [
                        below[:, at : at + size].reshape(shape),
                        g,
                        above[:, at : at + size].reshape(shape),
                    ],
                    axis=dim,
                )
            )
            at += size
        grids = out
    return grids


def shards(fine_multipoles, present, m2m_ops, m2l_ops, l2l_ops):
    points, width = fine_multipoles.shape
    local_bits = width.bit_length() - 1
    devices = lax.axis_size("box")
    device_bits = devices.bit_length() - 1
    nf, nc = width // 8, width // 64
    masked = jnp.where(present[None, :] > 0, fine_multipoles, jnp.zeros_like(fine_multipoles))
    fine = masked.reshape(points, nf, 8).transpose(2, 1, 0)
    coarse = jnp.einsum(
        "kcq,kpq->cp", fine, m2m_ops, preferred_element_type=jnp.float32
    ).astype(jnp.bfloat16)
    coarse = coarse.reshape(nc, 8, points).transpose(1, 0, 2)
    grids = exchange(
        [to_grid(fine, local_bits - 3), to_grid(coarse, local_bits - 6)],
        devices, device_bits, local_bits,
    )
    flat = [g.reshape(8, -1, points) for g in grids]
    rows = far_field(flat[0], flat[1], m2l_ops, l2l_ops, nf, nc, local_bits)
    out = rows.reshape(8, 8, nc, points).transpose(3, 2, 1, 0).reshape(points, width)
    return jnp.where(present[None, :] > 0, out, 0.0)


def solution(mesh):
    in_specs = (P(None, "box"), P("box"), P(), P(), P())
    out_specs = P(None, "box")
    return jax.shard_map(shards, mesh=mesh, in_specs=in_specs, out_specs=out_specs, check_vma=False)
```

```python
import functools

import jax
import jax.numpy as jnp
import numpy as np
from jax import lax
from jax.experimental import pallas as pl
from jax.experimental.pallas import tpu as pltpu
from jax.sharding import PartitionSpec as P

PAD = 16
GROUPS = ((8, 7), (4, 5), (2, 5), (1, 1))
SLABS = 8
NT_DIMS = (((1,), (1,)), ((), ()))


def offsets_table():
    entries = []
    for u in range(-3, 4):
        for v in range(-3, 4):
            for w in range(-3, 4):
                if max(abs(u), abs(v), abs(w)) >= 2:
                    entries.append((u, v, w))
    return entries


def coords_of(number, bit_count):
    out = [0, 0, 0]
    for i in range(bit_count):
        out[i % 3] |= (number >> i & 1) << (i // 3)
    return out


def extents(bit_count):
    return [2 ** len([i for i in range(bit_count) if i % 3 == a]) for a in range(3)]


def kind(o):
    return {-3: 0, 3: 2}.get(o, 1)


def classes_of(kinds):
    allowed = {0: (1,), 1: (0, 1), 2: (0,)}
    return [
        k
        for k in range(8)
        if all((k >> a & 1) in allowed[kinds[a]] for a in range(3))
    ]


def build_tables():
    offsets = offsets_table()
    tables = []
    for classes, together in GROUPS:
        rows = []
        for kinds in np.ndindex(3, 3, 3):
            ks = classes_of(kinds)
            if len(ks) != classes:
                continue
            members = [t for t, o in enumerate(offsets) if tuple(map(kind, o)) == kinds]
            for first in range(0, len(members), together):
                entry = list(ks)
                for t in members[first : first + together]:
                    entry.append(t)
                    for k in ks:
                        d, child = 0, 0
                        for a in range(3):
                            s = offsets[t][a] + (k >> a & 1)
                            child |= (s & 1) << a
                            d = d * 3 + (s >> 1) + 1
                        entry.append(d * 8 + child)
                rows.append(entry)
        tables.append(np.array(rows, np.int32))
    return tables


def selector(bit_count, pad):
    ex = extents(bit_count)
    count = 2**bit_count
    rows = max(count, pad)
    sel = np.zeros((27, rows, (ex[0] + 2) * (ex[1] + 2) * (ex[2] + 2)), np.float32)
    for c in range(count):
        x = coords_of(c, bit_count)
        r = (c & 7) * (count // 8) + (c >> 3) if count >= 64 else c
        for d in range(27):
            s = [x[0] + d // 9, x[1] + d // 3 % 3, x[2] + d % 3]
            sel[d, r, (s[0] * (ex[1] + 2) + s[1]) * (ex[2] + 2) + s[2]] = 1
    return sel.reshape(27 * rows, -1)


def far_kernel(
    layout, nf, nc, tab_ref, fine_ref, coarse_ref, sf_ref, sc_ref, l2l_ref, m2l_ref,
    out_ref, ops, win, acc, sems
):
    total = ops.shape[0]
    copies = []
    for i in range(SLABS):
        at, end = total * i // SLABS, total * (i + 1) // SLABS
        copy = pltpu.make_async_copy(
            m2l_ref.at[pl.ds(at, end - at)], ops.at[pl.ds(at, end - at)], sems.at[i]
        )
        copy.start()
        copies.append(copy)
    acc[...] = jnp.zeros_like(acc)

    def build(j, carry):
        f = fine_ref[j]
        c = coarse_ref[j]
        for d in range(0, 27, 9):
            part = jnp.dot(
                sf_ref[d * nf : (d + 9) * nf, :], f, preferred_element_type=jnp.float32
            ).astype(jnp.bfloat16)
            for e in range(9):
                win[(d + e) * 8 + j, 0:nf, :] = part[e * nf : (e + 1) * nf]
        part = jnp.dot(sc_ref[...], c, preferred_element_type=jnp.float32).astype(jnp.bfloat16)
        for d in range(27):
            win[d * 8 + j, nf : nf + PAD, :] = part[d * PAD : (d + 1) * PAD]
        return carry

    lax.fori_loop(0, 8, build, 0)
    rows = nf + PAD

    for copy in copies:
        copy.wait()

    def apply(base, classes, together):
        sums = None
        for j in range(together):
            at = base + classes + j * (classes + 1)
            lhs = [win[tab_ref[at + 1 + e]] for e in range(classes)]
            lhs = jnp.concatenate(lhs, axis=0) if classes > 1 else lhs[0]
            term = lax.dot_general(
                lhs, ops[tab_ref[at]], NT_DIMS, preferred_element_type=jnp.float32
            )
            sums = term if sums is None else sums + term
        for e in range(classes):
            acc[tab_ref[base + e]] += sums[e * rows : (e + 1) * rows]

    for first, count, width, classes, together in layout:

        def step(n, carry, first=first, width=width, classes=classes, together=together):
            apply(first + n * width, classes, together)
            return carry

        lax.fori_loop(0, count, step, 0)

    down = jnp.concatenate([acc[k, nf : nf + nc, :] for k in range(8)], axis=0).astype(jnp.bfloat16)
    for k in range(8):
        out_ref[k] = acc[k, 0:nf, :] + lax.dot_general(
            down, l2l_ref[k], NT_DIMS, preferred_element_type=jnp.float32
        )


def far_field(fine, coarse, m2l_ops, l2l_ops, nf, nc, local_bits):
    tables = build_tables()
    layout, at = [], 0
    for table, (classes, together) in zip(tables, GROUPS):
        layout.append((at,) + table.shape + (classes, together))
        at += table.size
    tab = np.concatenate([table.reshape(-1) for table in tables])
    points = fine.shape[-1]
    sf = jnp.asarray(selector(local_bits - 3, 0), jnp.bfloat16)
    sc = jnp.asarray(selector(local_bits - 6, PAD), jnp.bfloat16)
    vmem = pl.BlockSpec(memory_space=pltpu.VMEM)
    smem = pl.BlockSpec(memory_space=pltpu.SMEM)
    return pl.pallas_call(
        functools.partial(far_kernel, layout, nf, nc),
        out_shape=jax.ShapeDtypeStruct((8, nf, points), jnp.float32),
        in_specs=[smem, vmem, vmem, vmem, vmem, vmem, pl.BlockSpec(memory_space=pl.ANY)],
        out_specs=vmem,
        scratch_shapes=[
            pltpu.VMEM(m2l_ops.shape, jnp.bfloat16),
            pltpu.VMEM((27 * 8, nf + PAD, points), jnp.bfloat16),
            pltpu.VMEM((8, nf + PAD, points), jnp.float32),
            pltpu.SemaphoreType.DMA((SLABS,)),
        ],
        compiler_params=pltpu.CompilerParams(vmem_limit_bytes=60 * 2**20),
        name="far_field",
    )(jnp.asarray(tab), fine, coarse, sf, sc, l2l_ops, m2l_ops)


def to_grid(boxes, bit_count):
    bitwise = boxes.reshape((2,) * bit_count + boxes.shape[1:])
    order = []
    for a in range(3):
        order += [bit_count - 1 - i for i in range(bit_count) if i % 3 == a][::-1]
    order += [bit_count, bit_count + 1]
    return bitwise.transpose(order).reshape(extents(bit_count) + list(boxes.shape[1:]))


def halo_kernel(device_bits, local_bits, *refs):
    blocks, outs, grids = refs[0:2], refs[2:4], refs[4:6]
    send_sems, recv_sems = refs[6:8]
    me = lax.axis_index("box")
    ways = []
    for axis in range(3):
        members = [p for p in range(device_bits) if (local_bits + p) % 3 == axis]
        bits = [lax.rem(lax.div(me, 1 << p), 2) for p in members]
        here = sum((bit * (1 << n) for n, bit in enumerate(bits)), jnp.int32(0))
        size = 1 << len(members)

        def device_at(coord):
            out = me
            for n, p in enumerate(members):
                out = out + (lax.rem(lax.div(coord, 1 << n), 2) - bits[n]) * (1 << p)
            return out

        ways.append(
            (
                (here < size - 1, device_at(here + 1)),
                (here > 0, device_at(here + (size - 1))),
            )
        )
    for block, grid in zip(blocks, grids):
        grid[...] = jnp.zeros_like(grid)
        x, y, z = block.shape[:3]
        grid[1 : x + 1, 1 : y + 1, 1 : z + 1] = block[...]
    barrier = pltpu.get_barrier_semaphore()
    flat = [way for pair in ways for way in pair]
    for there, device in flat:

        @pl.when(there)
        def _(device=device):
            pl.semaphore_signal(
                barrier, inc=1, device_id=(device,), device_id_type=pl.DeviceIdType.MESH
            )

    peers = sum((jnp.where(there, 1, 0) for there, _ in flat), jnp.int32(0))
    pl.semaphore_wait(barrier, peers)

    for axis in range(3):
        moves = []
        for way in range(2):
            for n, grid in enumerate(grids):
                extent = [e - 2 for e in grid.shape[:3]]
                region = [
                    pl.ds(0, extent[a] + 2) if a < axis else pl.ds(1, extent[a]) for a in range(3)
                ]
                source, target = list(region), list(region)
                source[axis] = pl.ds(extent[axis] if way == 0 else 1, 1)
                target[axis] = pl.ds(0 if way == 0 else extent[axis] + 1, 1)
                at = (axis * 2 + way) * 2 + n
                copy = pltpu.make_async_remote_copy(
                    src_ref=grid.at[tuple(source)],
                    dst_ref=grid.at[tuple(target)],
                    send_sem=send_sems.at[at],
                    recv_sem=recv_sems.at[at],
                    device_id=(ways[axis][way][1],),
                    device_id_type=pl.DeviceIdType.MESH,
                )
                moves.append((way, copy))
        for way, copy in moves:
            pl.when(ways[axis][way][0])(copy.start)
        for way, copy in moves:
            pl.when(ways[axis][way][0])(copy.wait_send)
            pl.when(ways[axis][1 - way][0])(copy.wait_recv)
    for grid, out in zip(grids, outs):
        out[...] = grid[...]


def exchange(blocks, device_bits, local_bits):
    shapes = [tuple(e + 2 for e in b.shape[:3]) + b.shape[3:] for b in blocks]
    vmem = pl.BlockSpec(memory_space=pltpu.VMEM)
    return pl.pallas_call(
        functools.partial(halo_kernel, device_bits, local_bits),
        out_shape=[jax.ShapeDtypeStruct(shape, jnp.bfloat16) for shape in shapes],
        in_specs=[vmem, vmem],
        out_specs=[vmem, vmem],
        scratch_shapes=[pltpu.VMEM(shape, jnp.bfloat16) for shape in shapes]
        + [pltpu.SemaphoreType.DMA((12,)), pltpu.SemaphoreType.DMA((12,))],
        compiler_params=pltpu.CompilerParams(collective_id=0, has_side_effects=True),
        name="halo",
    )(*blocks)


def shards(fine_multipoles, present, m2m_ops, m2l_ops, l2l_ops):
    points, width = fine_multipoles.shape
    local_bits = width.bit_length() - 1
    devices = lax.axis_size("box")
    device_bits = devices.bit_length() - 1
    nf, nc = width // 8, width // 64
    masked = jnp.where(present[None, :] > 0, fine_multipoles, jnp.zeros_like(fine_multipoles))
    fine = masked.T.reshape(nf, 8, points)
    coarse = jnp.einsum(
        "ckq,kpq->cp", fine, m2m_ops, preferred_element_type=jnp.float32
    ).astype(jnp.bfloat16)
    grids = exchange(
        [to_grid(fine, local_bits - 3), to_grid(coarse.reshape(nc, 8, points), local_bits - 6)],
        device_bits, local_bits,
    )
    flat = [g.reshape(-1, 8, points).transpose(1, 0, 2) for g in grids]
    rows = far_field(flat[0], flat[1], m2l_ops, l2l_ops, nf, nc, local_bits)
    out = rows.reshape(8, 8, nc, points).transpose(3, 2, 1, 0).reshape(points, width)
    return jnp.where(present[None, :] > 0, out, 0.0)


def solution(mesh):
    in_specs = (P(None, "box"), P("box"), P(), P(), P())
    out_specs = P(None, "box")
    return jax.shard_map(shards, mesh=mesh, in_specs=in_specs, out_specs=out_specs, check_vma=False)
```

```python
import functools

import jax
import jax.numpy as jnp
import numpy as np
from jax import lax
from jax.experimental import pallas as pl
from jax.experimental.pallas import tpu as pltpu
from jax.sharding import PartitionSpec as P

PAD = 16
GROUPS = ((8, 7), (4, 5), (2, 5), (1, 1))
NT_DIMS = (((1,), (1,)), ((), ()))


def offsets_table():
    entries = []
    for u in range(-3, 4):
        for v in range(-3, 4):
            for w in range(-3, 4):
                if max(abs(u), abs(v), abs(w)) >= 2:
                    entries.append((u, v, w))
    return entries


def coords_of(number, bit_count):
    out = [0, 0, 0]
    for i in range(bit_count):
        out[i % 3] |= (number >> i & 1) << (i // 3)
    return out


def extents(bit_count):
    return [2 ** len([i for i in range(bit_count) if i % 3 == a]) for a in range(3)]


def kind(o):
    return {-3: 0, 3: 2}.get(o, 1)


def classes_of(kinds):
    allowed = {0: (1,), 1: (0, 1), 2: (0,)}
    return [
        k
        for k in range(8)
        if all((k >> a & 1) in allowed[kinds[a]] for a in range(3))
    ]


def build_tables():
    offsets = offsets_table()
    slabs = []
    for u in range(-3, 4):
        members = [t for t, o in enumerate(offsets) if o[0] == u]
        slabs.append((members[0], len(members)))
    steps = {(u, g): [] for u in range(7) for g in range(len(GROUPS))}
    for g, (classes, together) in enumerate(GROUPS):
        for kinds in np.ndindex(3, 3, 3):
            ks = classes_of(kinds)
            if len(ks) != classes:
                continue
            members = [t for t, o in enumerate(offsets) if tuple(map(kind, o)) == kinds]
            if classes < 8:
                members.sort(key=lambda t: (offsets[t][0], t))
            for first in range(0, len(members), together):
                entry = list(ks)
                for t in members[first : first + together]:
                    entry.append(t)
                    for k in ks:
                        d, child = 0, 0
                        for a in range(3):
                            s = offsets[t][a] + (k >> a & 1)
                            child |= (s & 1) << a
                            d = d * 3 + (s >> 1) + 1
                        entry.append(d * 8 + child)
                last = max(members[first : first + together])
                steps[offsets[last][0] + 3, g].append(entry)
    table, starts = [], []
    for key in sorted(steps):
        starts += [len(table), len(steps[key])]
        table += sum(steps[key], [])
    return np.array(table, np.int32), np.array(starts, np.int32), slabs


def selector(bit_count, pad):
    ex = extents(bit_count)
    count = 2**bit_count
    rows = max(count, pad)
    sel = np.zeros((27, rows, (ex[0] + 2) * (ex[1] + 2) * (ex[2] + 2)), np.float32)
    for c in range(count):
        x = coords_of(c, bit_count)
        r = (c & 7) * (count // 8) + (c >> 3) if count >= 64 else c
        for d in range(27):
            s = [x[0] + d // 9, x[1] + d // 3 % 3, x[2] + d % 3]
            sel[d, r, (s[0] * (ex[1] + 2) + s[1]) * (ex[2] + 2) + s[2]] = 1
    return sel.reshape(27 * rows, -1)


def far_kernel(
    slabs, nf, nc, tab_ref, start_ref, fine_ref, coarse_ref, sf_ref, sc_ref, l2l_ref, m2l_ref,
    out_ref, ops, win, acc, sems
):
    copies = []
    for i, (first, size) in enumerate(slabs):
        copy = pltpu.make_async_copy(
            m2l_ref.at[pl.ds(first, size)], ops.at[pl.ds(first, size)], sems.at[i]
        )
        copy.start()
        copies.append(copy)
    acc[...] = jnp.zeros_like(acc)

    def build(j, carry):
        f = fine_ref[j]
        c = coarse_ref[j]
        for d in range(0, 27, 9):
            part = jnp.dot(
                sf_ref[d * nf : (d + 9) * nf, :], f, preferred_element_type=jnp.float32
            ).astype(jnp.bfloat16)
            for e in range(9):
                win[(d + e) * 8 + j, 0:nf, :] = part[e * nf : (e + 1) * nf]
        part = jnp.dot(sc_ref[...], c, preferred_element_type=jnp.float32).astype(jnp.bfloat16)
        for d in range(27):
            win[d * 8 + j, nf : nf + PAD, :] = part[d * PAD : (d + 1) * PAD]
        return carry

    lax.fori_loop(0, 8, build, 0)
    rows = nf + PAD

    def apply(base, classes, together):
        sums = None
        for j in range(together):
            at = base + classes + j * (classes + 1)
            lhs = [win[tab_ref[at + 1 + e]] for e in range(classes)]
            lhs = jnp.concatenate(lhs, axis=0) if classes > 1 else lhs[0]
            term = lax.dot_general(
                lhs, ops[tab_ref[at]], NT_DIMS, preferred_element_type=jnp.float32
            )
            sums = term if sums is None else sums + term
        for e in range(classes):
            acc[tab_ref[base + e]] += sums[e * rows : (e + 1) * rows]

    def slab_body(slab, carry):
        for i, copy in enumerate(copies):
            pl.when(slab == i)(copy.wait)
        for g, (classes, together) in enumerate(GROUPS):
            at = (slab * len(GROUPS) + g) * 2
            first = start_ref[at]

            def step(n, carry, first=first, classes=classes, together=together):
                apply(first + n * (classes + together * (classes + 1)), classes, together)
                return carry

            lax.fori_loop(0, start_ref[at + 1], step, 0)
        return carry

    lax.fori_loop(0, len(slabs), slab_body, 0)

    down = jnp.concatenate([acc[k, nf : nf + nc, :] for k in range(8)], axis=0).astype(jnp.bfloat16)
    for k in range(8):
        out_ref[k] = acc[k, 0:nf, :] + lax.dot_general(
            down, l2l_ref[k], NT_DIMS, preferred_element_type=jnp.float32
        )


def far_field(fine, coarse, m2l_ops, l2l_ops, nf, nc, local_bits):
    tab, starts, slabs = build_tables()
    points = fine.shape[-1]
    sf = jnp.asarray(selector(local_bits - 3, 0), jnp.bfloat16)
    sc = jnp.asarray(selector(local_bits - 6, PAD), jnp.bfloat16)
    vmem = pl.BlockSpec(memory_space=pltpu.VMEM)
    smem = pl.BlockSpec(memory_space=pltpu.SMEM)
    return pl.pallas_call(
        functools.partial(far_kernel, slabs, nf, nc),
        out_shape=jax.ShapeDtypeStruct((8, nf, points), jnp.float32),
        in_specs=[smem, smem, vmem, vmem, vmem, vmem, vmem, pl.BlockSpec(memory_space=pl.ANY)],
        out_specs=vmem,
        scratch_shapes=[
            pltpu.VMEM(m2l_ops.shape, jnp.bfloat16),
            pltpu.VMEM((27 * 8, nf + PAD, points), jnp.bfloat16),
            pltpu.VMEM((8, nf + PAD, points), jnp.float32),
            pltpu.SemaphoreType.DMA((len(slabs),)),
        ],
        compiler_params=pltpu.CompilerParams(vmem_limit_bytes=60 * 2**20),
        name="far_field",
    )(jnp.asarray(tab), jnp.asarray(starts), fine, coarse, sf, sc, l2l_ops, m2l_ops)


def to_grid(boxes, bit_count):
    bitwise = boxes.reshape((2,) * bit_count + boxes.shape[1:])
    order = []
    for a in range(3):
        order += [bit_count - 1 - i for i in range(bit_count) if i % 3 == a][::-1]
    order += [bit_count, bit_count + 1]
    return bitwise.transpose(order).reshape(extents(bit_count) + list(boxes.shape[1:]))


def halo_kernel(device_bits, local_bits, *refs):
    blocks, outs, grids = refs[0:2], refs[2:4], refs[4:6]
    send_sems, recv_sems = refs[6:8]
    me = lax.axis_index("box")
    ways = []
    for axis in range(3):
        members = [p for p in range(device_bits) if (local_bits + p) % 3 == axis]
        bits = [lax.rem(lax.div(me, 1 << p), 2) for p in members]
        here = sum((bit * (1 << n) for n, bit in enumerate(bits)), jnp.int32(0))
        size = 1 << len(members)

        def device_at(coord):
            out = me
            for n, p in enumerate(members):
                out = out + (lax.rem(lax.div(coord, 1 << n), 2) - bits[n]) * (1 << p)
            return out

        ways.append(
            (
                (here < size - 1, device_at(here + 1)),
                (here > 0, device_at(here + (size - 1))),
            )
        )
    for block, grid in zip(blocks, grids):
        grid[...] = jnp.zeros_like(grid)
        x, y, z = block.shape[:3]
        grid[1 : x + 1, 1 : y + 1, 1 : z + 1] = block[...]
    barrier = pltpu.get_barrier_semaphore()
    flat = [way for pair in ways for way in pair]
    for there, device in flat:

        @pl.when(there)
        def _(device=device):
            pl.semaphore_signal(
                barrier, inc=1, device_id=(device,), device_id_type=pl.DeviceIdType.MESH
            )

    peers = sum((jnp.where(there, 1, 0) for there, _ in flat), jnp.int32(0))
    pl.semaphore_wait(barrier, peers)

    for axis in range(3):
        moves = []
        for way in range(2):
            for n, grid in enumerate(grids):
                extent = [e - 2 for e in grid.shape[:3]]
                region = [
                    pl.ds(0, extent[a] + 2) if a < axis else pl.ds(1, extent[a]) for a in range(3)
                ]
                source, target = list(region), list(region)
                source[axis] = pl.ds(extent[axis] if way == 0 else 1, 1)
                target[axis] = pl.ds(0 if way == 0 else extent[axis] + 1, 1)
                at = (axis * 2 + way) * 2 + n
                copy = pltpu.make_async_remote_copy(
                    src_ref=grid.at[tuple(source)],
                    dst_ref=grid.at[tuple(target)],
                    send_sem=send_sems.at[at],
                    recv_sem=recv_sems.at[at],
                    device_id=(ways[axis][way][1],),
                    device_id_type=pl.DeviceIdType.MESH,
                )
                moves.append((way, copy))
        for way, copy in moves:
            pl.when(ways[axis][way][0])(copy.start)
        for way, copy in moves:
            pl.when(ways[axis][way][0])(copy.wait_send)
            pl.when(ways[axis][1 - way][0])(copy.wait_recv)
    for grid, out in zip(grids, outs):
        out[...] = grid[...]


def exchange(blocks, device_bits, local_bits):
    shapes = [tuple(e + 2 for e in b.shape[:3]) + b.shape[3:] for b in blocks]
    vmem = pl.BlockSpec(memory_space=pltpu.VMEM)
    return pl.pallas_call(
        functools.partial(halo_kernel, device_bits, local_bits),
        out_shape=[jax.ShapeDtypeStruct(shape, jnp.bfloat16) for shape in shapes],
        in_specs=[vmem, vmem],
        out_specs=[vmem, vmem],
        scratch_shapes=[pltpu.VMEM(shape, jnp.bfloat16) for shape in shapes]
        + [pltpu.SemaphoreType.DMA((12,)), pltpu.SemaphoreType.DMA((12,))],
        compiler_params=pltpu.CompilerParams(collective_id=0, has_side_effects=True),
        name="halo",
    )(*blocks)


def shards(fine_multipoles, present, m2m_ops, m2l_ops, l2l_ops):
    points, width = fine_multipoles.shape
    local_bits = width.bit_length() - 1
    devices = lax.axis_size("box")
    device_bits = devices.bit_length() - 1
    nf, nc = width // 8, width // 64
    masked = jnp.where(present[None, :] > 0, fine_multipoles, jnp.zeros_like(fine_multipoles))
    fine = masked.T.reshape(nf, 8, points)
    coarse = jnp.einsum(
        "ckq,kpq->cp", fine, m2m_ops, preferred_element_type=jnp.float32
    ).astype(jnp.bfloat16)
    grids = exchange(
        [to_grid(fine, local_bits - 3), to_grid(coarse.reshape(nc, 8, points), local_bits - 6)],
        device_bits, local_bits,
    )
    flat = [g.reshape(-1, 8, points).transpose(1, 0, 2) for g in grids]
    rows = far_field(flat[0], flat[1], m2l_ops, l2l_ops, nf, nc, local_bits)
    out = rows.reshape(8, 8, nc, points).transpose(3, 2, 1, 0).reshape(points, width)
    return jnp.where(present[None, :] > 0, out, 0.0)


def solution(mesh):
    in_specs = (P(None, "box"), P("box"), P(), P(), P())
    out_specs = P(None, "box")
    return jax.shard_map(shards, mesh=mesh, in_specs=in_specs, out_specs=out_specs, check_vma=False)
```
